32 devices in a mesh: ctx: 8 (over z, core), chan: 4 (over y, x).
Axes of the slice: x: 2, y: 2, z: 4, core: 2. Of those that a mesh axis runs over, the one named last changes fastest.
Arguments:
- frames: bfloat16 [2, 9216, 1536], P(None, 'ctx'), may hold values from -6 to 6
- ln_gain: float32 [1536], replicated, may hold values from 0.5 to 1.5
- ln_bias: float32 [1536], replicated, may hold values from -3 to 3
- w_in: bfloat16 [1536, 2, 1536], P('ctx', None, 'chan'), may hold values from -0.15625 to 0.15625
- w_depth: float32 [31, 1536], P(None, 'chan'), may hold values from -1 to 1
- bn_gain: float32 [1536], P('chan'), may hold values from 0.1 to 1.9
- bn_bias: float32 [1536], P('chan'), may hold values from -3 to 3
- w_out: bfloat16 [1536, 1536], P('ctx', 'chan'), may hold values from -0.15625 to 0.15625
- lengths: int32 [2], replicated, may hold values from 2304 to 9216, as said below
- grad_out: bfloat16 [2, 9216, 1536], P(None, 'ctx'), may hold values from -6 to 6
Outputs:
- block_out: bfloat16 [2, 9216, 1536], P(None, 'ctx', 'chan')
- grad_frames: bfloat16 [2, 9216, 1536], P(None, 'ctx', 'chan')
- grad_w_in: float32 [1536, 2, 1536], P('ctx', None, 'chan')
- grad_w_out: float32 [1536, 1536], P('ctx', 'chan')
- grad_w_depth: float32 [31, 1536], P(None, 'chan')
- grad_bn: float32 [2, 1536], P(None, 'chan')
- grad_ln: float32 [2, 1536], P(None, 'chan')
The draws below stay inside these ranges and needn't reach their ends.
Inputs may be any that keep to these rules, and one draw needn't show every extreme that they name: `lengths`: recording 0 always has all 9216 frames valid.
All inputs are finite; a program needn't handle non-finite values.
Results may differ from the reference program's by a relative error of at most 0.018.
Values may be sent and summed in bfloat16 or wider, within the bound.
A program may use at most 192 MiB of HBM per device.

```python
import jax
import jax.numpy as jnp
from jax import lax

D = 1536
K = 31
B = 2
SEQ = 9216


def draw_lengths(key, part):
    others = jax.random.randint(key, (B,), SEQ // 4, SEQ + 1, dtype=jnp.int32)
    leading = jnp.arange(B, dtype=jnp.int32) == 0
    return jnp.where(leading, SEQ, others).astype(jnp.int32)


def level_of(key, shape, pieces, least, top_value):
    def one(dim, blocks):
        draws = jax.random.uniform(jax.random.fold_in(jax.random.fold_in(key, 6), dim), (blocks,), jnp.float32, least / len(pieces), top_value / len(pieces))
        return jnp.repeat(jnp.exp(draws), shape[dim] // blocks).reshape((-1,) + (1,) * (len(shape) - dim - 1))

    loudness = one(*pieces[0])
    for cut in pieces[1:]:
        loudness = loudness * one(*cut)
    return loudness


def bell_draw(own_key, dims, scale, most, cuts=(), held_as=jnp.bfloat16):
    gain = level_of(own_key, dims, cuts, -0.22, 0.18) if cuts else 1.0
    values = jax.random.normal(own_key, dims, jnp.float32) * scale * gain
    return jnp.minimum(jnp.maximum(values, -most), most).astype(held_as)


def setup_inputs(seed: int = 0) -> dict:
    splits = jax.random.split(jax.random.key(seed), 11)
    frames = bell_draw(splits[0], (B, SEQ, D), 1.0, 6.0, ((1, 8),))
    ln_gain = jnp.clip(1.0 + 0.1 * jax.random.normal(splits[1], (D,), jnp.float32), 0.5, 1.5)
    ln_bias = bell_draw(splits[2], (D,), 0.5, 3.0, (), jnp.float32)
    w_in = bell_draw(splits[3], (D, 2, D), D ** -0.5, 0.15625, ((0, 8), (2, 4)))
    w_depth = bell_draw(splits[4], (K, D), K ** -0.5, 1.0, ((1, 4),), jnp.float32)
    bn_gain = jnp.clip(1.0 + 0.18 * jax.random.normal(splits[5], (D,), jnp.float32), 0.1, 1.9)
    bn_bias = bell_draw(splits[6], (D,), 0.5, 3.0, ((0, 4),), jnp.float32)
    w_out = bell_draw(splits[7], (D, D), D ** -0.5, 0.15625, ((0, 8), (1, 4)))
    lengths = draw_lengths(jax.random.fold_in(splits[10], 71), 0)
    grad_out = bell_draw(splits[9], (B, SEQ, D), 1.0, 6.0, ((1, 8),))
    return dict(frames=frames, ln_gain=ln_gain, ln_bias=ln_bias, w_in=w_in, w_depth=w_depth, bn_gain=bn_gain, bn_bias=bn_bias, w_out=w_out, lengths=lengths, grad_out=grad_out)


epsilon = 1e-05

def frame_mask(lengths, length):
    position = jnp.arange(length, dtype=jnp.int32)
    return (position[None, :] < lengths[:, None]).astype(jnp.float32)[:, :, None]

def reference(frames, ln_gain, ln_bias, w_in, w_depth, bn_gain, bn_bias, w_out, lengths, grad_out):
    records, length, model_width = frames.shape
    tap_count = w_depth.shape[0]
    margin = (tap_count - 1) // 2
    total_rows = records * length
    valid_mask = frame_mask(lengths, length)
    frame_count = jnp.sum(lengths.astype(jnp.float32))
    inputs = frames.astype(jnp.float32)
    centred = inputs - lax.optimization_barrier(jnp.mean(inputs, axis=-1, keepdims=True))
    ln_rstd = lax.rsqrt(lax.optimization_barrier(jnp.mean(centred * centred, axis=-1, keepdims=True)) + epsilon)
    ln_hat = centred * ln_rstd
    normed = (ln_hat * ln_gain + ln_bias).astype(jnp.bfloat16)
    normed_rows = normed.reshape(total_rows, model_width)
    w_in_flat = w_in.reshape(model_width, 2 * model_width)
    projected = jnp.dot(normed_rows, w_in_flat, preferred_element_type=jnp.float32)
    projected = projected.reshape(records, length, 2, model_width)
    values = projected[:, :, 0]
    gate_vals = jax.nn.sigmoid(projected[:, :, 1])
    glu_out = (values * gate_vals * valid_mask).astype(jnp.bfloat16)
    padded = jnp.pad(glu_out.astype(jnp.float32), ((0, 0), (margin, margin), (0, 0)))
    depth_out = jnp.zeros((records, length, model_width), jnp.float32)
    for offset in range(tap_count):
        depth_out = depth_out + padded[:, offset:offset + length] * w_depth[offset]
    bn_mean = lax.optimization_barrier(jnp.sum(depth_out * valid_mask, axis=(0, 1))) / frame_count
    bn_cent = (depth_out - bn_mean) * valid_mask
    bn_rstd = lax.rsqrt(lax.optimization_barrier(jnp.sum(bn_cent * bn_cent, axis=(0, 1))) / frame_count + epsilon)
    bn_hat = (depth_out - bn_mean) * bn_rstd
    bn_out = bn_hat * bn_gain + bn_bias
    swish_gate = jax.nn.sigmoid(bn_out)
    activated = (bn_out * swish_gate * valid_mask).astype(jnp.bfloat16)
    act_rows = activated.reshape(total_rows, model_width)
    proj_out = lax.dot_general(act_rows, w_out, (((1,), (1,)), ((), ())), preferred_element_type=jnp.float32)
    block_out = (inputs.reshape(total_rows, model_width) + proj_out).astype(jnp.bfloat16)
    block_out = block_out.reshape(records, length, model_width)
    grad_rows = grad_out.reshape(total_rows, model_width)
    grad_w_out = lax.dot_general(grad_rows, act_rows, (((0,), (0,)), ((), ())), preferred_element_type=jnp.float32)
    grad_act = jnp.dot(grad_rows, w_out, preferred_element_type=jnp.float32).reshape(records, length, model_width)
    grad_bn_out = grad_act * valid_mask * (swish_gate * (1.0 + bn_out * (1.0 - swish_gate)))
    gain_sum = lax.optimization_barrier(jnp.sum(grad_bn_out * bn_hat, axis=(0, 1)))
    bias_sum = lax.optimization_barrier(jnp.sum(grad_bn_out, axis=(0, 1)))
    grad_depth = valid_mask * (bn_gain * bn_rstd) * (grad_bn_out - (bias_sum + bn_hat * gain_sum) / frame_count)
    grad_w_depth = jnp.stack([lax.optimization_barrier(jnp.sum(grad_depth * padded[:, offset:offset + length], axis=(0, 1))) for offset in range(tap_count)])
    grad_padded = jnp.pad(grad_depth, ((0, 0), (margin, margin), (0, 0)))
    grad_glu = jnp.zeros((records, length, model_width), jnp.float32)
    for offset in range(tap_count):
        begin_at = tap_count - 1 - offset
        grad_glu = grad_glu + grad_padded[:, begin_at:begin_at + length] * w_depth[offset]
    grad_glu = grad_glu * valid_mask
    grad_values = grad_glu * gate_vals
    grad_gates = grad_glu * values * gate_vals * (1.0 - gate_vals)
    grad_proj = jnp.stack([grad_values, grad_gates], axis=2).astype(jnp.bfloat16).reshape(total_rows, 2 * model_width)
    grad_w_in = lax.dot_general(normed_rows, grad_proj, (((0,), (0,)), ((), ())), preferred_element_type=jnp.float32)
    grad_w_in = grad_w_in.reshape(model_width, 2, model_width)
    grad_normed = lax.dot_general(grad_proj, w_in_flat, (((1,), (1,)), ((), ())), preferred_element_type=jnp.float32)
    grad_normed = grad_normed.reshape(records, length, model_width)
    grad_ln = jnp.stack([lax.optimization_barrier(jnp.sum(grad_normed * ln_hat, axis=(0, 1))), lax.optimization_barrier(jnp.sum(grad_normed, axis=(0, 1)))])
    scaled = grad_normed * ln_gain
    first_mean = lax.optimization_barrier(jnp.mean(scaled, axis=-1, keepdims=True))
    second_mean = lax.optimization_barrier(jnp.mean(scaled * ln_hat, axis=-1, keepdims=True))
    grad_frames = (ln_rstd * (scaled - first_mean - ln_hat * second_mean) + grad_out.astype(jnp.float32)).astype(jnp.bfloat16)
    grad_bn = jnp.stack([gain_sum, bias_sum])
    return (block_out, grad_frames, grad_w_in, grad_w_out, grad_w_depth, grad_bn, grad_ln)
```

```python
import functools

import jax
import jax.numpy as jnp
from jax import lax
from jax.experimental import pallas as pl
from jax.experimental.pallas import tpu as pltpu
from jax.sharding import PartitionSpec as P

epsilon = 1e-05


def padded_2(shard, sides, width):
    for axis, dim in sides:
        devices, length = (lax.axis_size(axis), shard.shape[dim])
        up = [(i, (i + 1) % devices) for i in range(devices - 1)]
        down = [(j, i) for i, j in up]
        last = lax.slice_in_dim(shard, length - width, length, axis=dim)
        initial = lax.slice_in_dim(shard, 0, width, axis=dim)
        before = lax.ppermute(last, axis, up)
        after = lax.ppermute(initial, axis, down)
        shard = jnp.concatenate([before, shard, after], axis=dim)
    return shard


def contract(left_op, right_op, left_dim, right_dim):
    return lax.dot_general(
        left_op,
        right_op,
        (((left_dim,), (right_dim,)), ((), ())),
        preferred_element_type=jnp.float32,
    )


def exchange_kernel(axes, summed, *refs):
    count = len(axes)
    inputs, outputs, slots = refs[:count], refs[count : 2 * count], refs[2 * count : 3 * count]
    send_sem, recv_sem = refs[3 * count :]
    barrier = pltpu.get_barrier_semaphore()
    greeted = 0
    for axis in sorted(set(axes)):
        devices, me = lax.axis_size(axis), lax.axis_index(axis)
        for step in range(1, devices):
            pl.semaphore_signal(
                barrier,
                inc=1,
                device_id={axis: lax.rem(me + step, devices)},
                device_id_type=pl.DeviceIdType.MESH,
            )
            greeted += 1
    pl.semaphore_wait(barrier, greeted)
    copies = []
    for axis, source, landing in zip(axes, inputs, slots):
        devices, me = lax.axis_size(axis), lax.axis_index(axis)
        for step in range(1, devices):
            copy = pltpu.make_async_remote_copy(
                src_ref=source,
                dst_ref=landing.at[me],
                send_sem=send_sem.at[len(copies)],
                recv_sem=recv_sem.at[len(copies)],
                device_id={axis: lax.rem(me + step, devices)},
                device_id_type=pl.DeviceIdType.MESH,
            )
            copy.start()
            copies.append(copy)
    for axis, source, landing in zip(axes, inputs, slots):
        landing[lax.axis_index(axis)] = source[...]
    for copy in copies:
        copy.wait_recv()
    for add_up, landing, output in zip(summed, slots, outputs):
        if add_up:
            total = landing[0]
            for place in range(1, landing.shape[0]):
                total = total + landing[place]
            output[...] = total
        else:
            output[...] = landing[...]
    for copy in copies:
        copy.wait_send()


def exchange(collective_id, *operands):
    arrays = [array for array, _, _ in operands]
    axes = tuple(axis for _, axis, _ in operands)
    summed = tuple(add_up for _, _, add_up in operands)
    stacked = [(lax.axis_size(axis),) + array.shape for array, axis, _ in operands]
    copies = sum(lax.axis_size(axis) - 1 for axis in axes)
    vmem = pl.BlockSpec(memory_space=pltpu.VMEM)
    return pl.pallas_call(
        functools.partial(exchange_kernel, axes, summed),
        out_shape=[
            jax.ShapeDtypeStruct(array.shape if add_up else shape, array.dtype)
            for array, shape, add_up in zip(arrays, stacked, summed)
        ],
        in_specs=[vmem] * len(arrays),
        out_specs=[vmem] * len(arrays),
        scratch_shapes=[
            pltpu.VMEM(shape, array.dtype) for array, shape in zip(arrays, stacked)
        ]
        + [pltpu.SemaphoreType.DMA((copies,)), pltpu.SemaphoreType.DMA((copies,))],
        compiler_params=pltpu.CompilerParams(collective_id=collective_id, has_side_effects=True),
    )(*arrays)


def scatter_sum(whole, axis):
    devices, me = lax.axis_size(axis), lax.axis_index(axis)
    chips, core, chip = devices // 2, lax.rem(me, 2), me // 2
    pieces = whole.reshape((chips, 2, whole.shape[0] // devices) + whole.shape[1:])
    kept = lax.dynamic_index_in_dim(pieces, core, 1, keepdims=False)
    sent = lax.dynamic_index_in_dim(pieces, 1 - core, 1, keepdims=False)
    got = lax.ppermute(sent, axis, [(i, i ^ 1) for i in range(devices)])
    pair = kept.astype(jnp.float32) + got.astype(jnp.float32)
    total = lax.dynamic_index_in_dim(pair, chip, 0, keepdims=False)
    rounded = pair.astype(jnp.bfloat16)
    for step in range(1, chips):
        part = lax.dynamic_index_in_dim(rounded, lax.rem(chip + step, chips), 0, keepdims=False)
        ring = [(i, ((i // 2 + step) % chips) * 2 + i % 2) for i in range(devices)]
        total = total + lax.ppermute(part, axis, ring).astype(jnp.float32)
    return total


def on_device(frames, ln_gain, ln_bias, w_in, w_depth, bn_gain, bn_bias, w_out, lengths, grad_out):
    records, local_len, model_width = frames.shape
    shard_in = w_in.shape[0]
    channels = w_in.shape[2]
    tap_count = w_depth.shape[0]
    margin = (tap_count - 1) // 2
    width = -(-margin // 16) * 16
    first_tap = width - margin
    local_rows = records * local_len
    chan_start = lax.axis_index("chan") * channels
    position = lax.axis_index("ctx") * local_len + jnp.arange(local_len, dtype=jnp.int32)
    valid_mask = (position[None, :] < lengths[:, None]).astype(jnp.float32)[:, :, None]
    frame_count = jnp.sum(lengths.astype(jnp.float32))
    inputs = frames.astype(jnp.float32)
    ln_mean = jnp.mean(inputs, axis=-1, keepdims=True)
    centred = inputs - ln_mean
    ln_rstd = lax.rsqrt(jnp.mean(centred * centred, axis=-1, keepdims=True) + epsilon)
    ln_hat = centred * ln_rstd
    normed = (ln_hat * ln_gain + ln_bias).astype(jnp.bfloat16)
    normed_rows = normed.reshape(local_rows, model_width)
    w_in_all = lax.all_gather(
        w_in.reshape(shard_in, 2 * channels), "ctx", axis=0, tiled=True
    )
    projected = jnp.dot(normed_rows, w_in_all, preferred_element_type=jnp.float32)
    projected = projected.reshape(records, local_len, 2, channels)
    values = projected[:, :, 0]
    gate_vals = jax.nn.sigmoid(projected[:, :, 1])
    glu_out = (values * gate_vals * valid_mask).astype(jnp.bfloat16)
    padded = padded_2(glu_out, (("ctx", 1),), width)
    depth_out = jnp.zeros((records, local_len, channels), jnp.float32)
    for offset in range(tap_count):
        at = first_tap + offset
        depth_out = depth_out + padded[:, at : at + local_len].astype(jnp.float32) * w_depth[offset]
    starts = jnp.arange(lax.axis_size("ctx"), dtype=jnp.int32) * local_len
    counts = jnp.sum(
        jnp.clip(lengths[None, :] - starts[:, None], 0, local_len).astype(jnp.float32), axis=1
    )
    own_count = jnp.maximum(
        jnp.sum(jnp.clip(lengths - starts[0] - lax.axis_index("ctx") * local_len, 0, local_len)), 1
    ).astype(jnp.float32)
    own_sum = jnp.sum(depth_out * valid_mask, axis=(0, 1))
    own_cent = (depth_out - own_sum / own_count) * valid_mask
    own_square = jnp.sum(own_cent * own_cent, axis=(0, 1))
    (stats,) = exchange(0, (jnp.stack([own_sum, own_square]), "ctx", False))
    sums, squares = stats[:, 0], stats[:, 1]
    bn_mean = jnp.sum(sums, axis=0) / frame_count
    shifts = sums / jnp.maximum(counts, 1.0)[:, None] - bn_mean
    bn_var = jnp.sum(squares + counts[:, None] * shifts * shifts, axis=0) / frame_count
    bn_rstd = lax.rsqrt(bn_var + epsilon)
    bn_hat = (depth_out - bn_mean) * bn_rstd
    bn_out = bn_hat * bn_gain + bn_bias
    swish_gate = jax.nn.sigmoid(bn_out)
    activated = (bn_out * swish_gate * valid_mask).astype(jnp.bfloat16)
    act_rows = activated.reshape(local_rows, channels)
    w_out_all = lax.all_gather(w_out, "ctx", axis=0, tiled=True)
    grad_rows = grad_out.reshape(local_rows, model_width)
    proj_out = contract(w_out_all, act_rows, 1, 1).astype(jnp.bfloat16)
    proj_out, late_grad = lax.optimization_barrier((proj_out, grad_rows))
    own_out = lax.psum_scatter(proj_out, "chan", scatter_dimension=0, tiled=True).T
    own_frames = lax.dynamic_slice_in_dim(
        frames.reshape(local_rows, model_width), chan_start, channels, 1
    ).astype(jnp.float32)
    block_out = (own_frames + own_out.astype(jnp.float32)).astype(jnp.bfloat16)
    block_out = block_out.reshape(records, local_len, channels)
    grad_act = jnp.dot(late_grad, w_out_all, preferred_element_type=jnp.float32)
    grad_act = grad_act.reshape(records, local_len, channels)
    grad_bn_out = grad_act * valid_mask * (swish_gate * (1.0 + bn_out * (1.0 - swish_gate)))
    own_grad_bn = jnp.stack(
        [jnp.sum(grad_bn_out * bn_hat, axis=(0, 1)), jnp.sum(grad_bn_out, axis=(0, 1))]
    )
    (grad_bn,) = exchange(1, (own_grad_bn, "ctx", True))
    gain_sum, bias_sum = grad_bn[0], grad_bn[1]
    grad_depth = (
        valid_mask
        * (bn_gain * bn_rstd)
        * (grad_bn_out - (bias_sum + bn_hat * gain_sum) / frame_count)
    )
    grad_padded = padded_2(grad_depth, (("ctx", 1),), width)
    grad_glu = jnp.zeros((records, local_len, channels), jnp.float32)
    for offset in range(tap_count):
        at = first_tap + tap_count - 1 - offset
        grad_glu = grad_glu + grad_padded[:, at : at + local_len] * w_depth[offset]
    grad_glu = grad_glu * valid_mask
    grad_values = grad_glu * gate_vals
    grad_gates = grad_glu * values * gate_vals * (1.0 - gate_vals)
    grad_proj = jnp.concatenate(
        [
            grad_values.astype(jnp.bfloat16).reshape(local_rows, channels),
            grad_gates.astype(jnp.bfloat16).reshape(local_rows, channels),
        ],
        axis=1,
    )
    grad_part = contract(w_in_all, grad_proj, 1, 1).astype(jnp.bfloat16)
    grad_part, act_rows, normed_rows, grad_proj, grad_depth, padded = lax.optimization_barrier(
        (grad_part, act_rows, normed_rows, grad_proj, grad_depth, padded)
    )
    own_grad = lax.psum_scatter(grad_part, "chan", scatter_dimension=0, tiled=True)
    own_grad = own_grad.T.astype(jnp.float32)
    grad_w_in = scatter_sum(contract(normed_rows, grad_proj, 0, 0).astype(jnp.bfloat16), "ctx")
    grad_w_in = grad_w_in.reshape(shard_in, 2, channels)
    grad_w_out = scatter_sum(contract(grad_rows, act_rows, 0, 0).astype(jnp.bfloat16), "ctx")
    depth_local = jnp.stack(
        [
            jnp.sum(
                grad_depth
                * padded[:, first_tap + offset : first_tap + offset + local_len].astype(jnp.float32),
                axis=(0, 1),
            )
            for offset in range(tap_count)
        ]
    )
    (grad_w_depth,) = exchange(2, (depth_local, "ctx", True))
    rstd_rows = ln_rstd.reshape(local_rows, 1)
    own_hat = (own_frames - ln_mean.reshape(local_rows, 1)) * rstd_rows
    own_gain = lax.dynamic_slice_in_dim(ln_gain, chan_start, channels, 0)
    own_scaled = own_grad * own_gain
    row_sums, grad_ln = exchange(
        3,
        (jnp.stack([jnp.sum(own_scaled, axis=1), jnp.sum(own_scaled * own_hat, axis=1)]), "chan", True),
        (jnp.stack([jnp.sum(own_grad * own_hat, axis=0), jnp.sum(own_grad, axis=0)]), "ctx", True),
    )
    first_rows, second_rows = row_sums[0], row_sums[1]
    own_dx = rstd_rows * (
        own_scaled
        - first_rows[:, None] / model_width
        - own_hat * (second_rows[:, None] / model_width)
    )
    own_cotangent = lax.dynamic_slice_in_dim(grad_rows, chan_start, channels, 1).astype(jnp.float32)
    grad_frames = (
        (own_dx + own_cotangent).astype(jnp.bfloat16).reshape(records, local_len, channels)
    )
    return (block_out, grad_frames, grad_w_in, grad_w_out, grad_w_depth, grad_bn, grad_ln)


def solution(mesh):
    in_specs = (
        P(None, "ctx", None),
        P(),
        P(),
        P("ctx", None, "chan"),
        P(None, "chan"),
        P("chan"),
        P("chan"),
        P("ctx", "chan"),
        P(),
        P(None, "ctx", None),
    )
    out_specs = (
        P(None, "ctx", "chan"),
        P(None, "ctx", "chan"),
        P("ctx", None, "chan"),
        P("ctx", "chan"),
        P(None, "chan"),
        P(None, "chan"),
        P(None, "chan"),
    )
    return jax.shard_map(
        on_device, mesh=mesh, in_specs=in_specs, out_specs=out_specs, check_vma=False
    )
```

```python
import functools

import jax
import jax.numpy as jnp
from jax import lax
from jax.experimental import pallas as pl
from jax.experimental.pallas import tpu as pltpu
from jax.sharding import PartitionSpec as P

epsilon = 1e-05


def padded_2(shard, sides, width):
    for axis, dim in sides:
        devices, length = (lax.axis_size(axis), shard.shape[dim])
        up = [(i, (i + 1) % devices) for i in range(devices - 1)]
        down = [(j, i) for i, j in up]
        last = lax.slice_in_dim(shard, length - width, length, axis=dim)
        initial = lax.slice_in_dim(shard, 0, width, axis=dim)
        before = lax.ppermute(last, axis, up)
        after = lax.ppermute(initial, axis, down)
        shard = jnp.concatenate([before, shard, after], axis=dim)
    return shard


def contract(left_op, right_op, left_dim, right_dim):
    return lax.dot_general(
        left_op,
        right_op,
        (((left_dim,), (right_dim,)), ((), ())),
        preferred_element_type=jnp.float32,
    )


def exchange_kernel(axes, summed, *refs):
    count = len(axes)
    inputs, outputs, slots = refs[:count], refs[count : 2 * count], refs[2 * count : 3 * count]
    send_sem, recv_sem = refs[3 * count :]
    barrier = pltpu.get_barrier_semaphore()
    greeted = 0
    for axis in sorted(set(axes)):
        devices, me = lax.axis_size(axis), lax.axis_index(axis)
        for step in range(1, devices):
            pl.semaphore_signal(
                barrier,
                inc=1,
                device_id={axis: lax.rem(me + step, devices)},
                device_id_type=pl.DeviceIdType.MESH,
            )
            greeted += 1
    pl.semaphore_wait(barrier, greeted)
    copies = []
    for axis, source, landing in zip(axes, inputs, slots):
        devices, me = lax.axis_size(axis), lax.axis_index(axis)
        for step in range(1, devices):
            copy = pltpu.make_async_remote_copy(
                src_ref=source,
                dst_ref=landing.at[me],
                send_sem=send_sem.at[len(copies)],
                recv_sem=recv_sem.at[len(copies)],
                device_id={axis: lax.rem(me + step, devices)},
                device_id_type=pl.DeviceIdType.MESH,
            )
            copy.start()
            copies.append(copy)
    for axis, source, landing in zip(axes, inputs, slots):
        landing[lax.axis_index(axis)] = source[...]
    for copy in copies:
        copy.wait_recv()
    for add_up, landing, output in zip(summed, slots, outputs):
        if add_up:
            total = landing[0]
            for place in range(1, landing.shape[0]):
                total = total + landing[place]
            output[...] = total
        else:
            output[...] = landing[...]
    for copy in copies:
        copy.wait_send()


def exchange(collective_id, *operands):
    arrays = [array for array, _, _ in operands]
    axes = tuple(axis for _, axis, _ in operands)
    summed = tuple(add_up for _, _, add_up in operands)
    stacked = [(lax.axis_size(axis),) + array.shape for array, axis, _ in operands]
    copies = sum(lax.axis_size(axis) - 1 for axis in axes)
    vmem = pl.BlockSpec(memory_space=pltpu.VMEM)
    return pl.pallas_call(
        functools.partial(exchange_kernel, axes, summed),
        out_shape=[
            jax.ShapeDtypeStruct(array.shape if add_up else shape, array.dtype)
            for array, shape, add_up in zip(arrays, stacked, summed)
        ],
        in_specs=[vmem] * len(arrays),
        out_specs=[vmem] * len(arrays),
        scratch_shapes=[
            pltpu.VMEM(shape, array.dtype) for array, shape in zip(arrays, stacked)
        ]
        + [pltpu.SemaphoreType.DMA((copies,)), pltpu.SemaphoreType.DMA((copies,))],
        compiler_params=pltpu.CompilerParams(collective_id=collective_id, has_side_effects=True),
    )(*arrays)


def scatter_sum(whole, axis):
    devices, me = lax.axis_size(axis), lax.axis_index(axis)
    chips, core, chip = devices // 2, lax.rem(me, 2), me // 2
    pieces = whole.reshape((chips, 2, whole.shape[0] // devices) + whole.shape[1:])
    kept = lax.dynamic_index_in_dim(pieces, core, 1, keepdims=False)
    sent = lax.dynamic_index_in_dim(pieces, 1 - core, 1, keepdims=False)
    got = lax.ppermute(sent, axis, [(i, i ^ 1) for i in range(devices)])
    pair = kept.astype(jnp.float32) + got.astype(jnp.float32)
    total = lax.dynamic_index_in_dim(pair, chip, 0, keepdims=False)
    rounded = pair.astype(jnp.bfloat16)
    for step in range(1, chips):
        part = lax.dynamic_index_in_dim(rounded, lax.rem(chip + step, chips), 0, keepdims=False)
        ring = [(i, ((i // 2 + step) % chips) * 2 + i % 2) for i in range(devices)]
        total = total + lax.ppermute(part, axis, ring).astype(jnp.float32)
    return total


def gather_rows(shard, axis):
    devices, me = lax.axis_size(axis), lax.axis_index(axis)
    chips, core, chip = devices // 2, lax.rem(me, 2), me // 2
    own = jnp.zeros((chips,) + shard.shape, shard.dtype)
    own = lax.dynamic_update_index_in_dim(own, shard, chip, 0)
    for step in range(1, chips):
        ring = [(i, ((i // 2 + step) % chips) * 2 + i % 2) for i in range(devices)]
        got = lax.ppermute(shard, axis, ring)
        own = lax.dynamic_update_index_in_dim(own, got, lax.rem(chip + chips - step, chips), 0)
    other = lax.ppermute(own, axis, [(i, i ^ 1) for i in range(devices)])
    whole = jnp.stack(
        [jnp.where(core == 0, own, other), jnp.where(core == 0, other, own)], axis=1
    )
    return whole.reshape((devices * shard.shape[0],) + shard.shape[1:])


def piece_kernel(weight_ref, rows_ref, out_ref):
    out_ref[...] = contract(rows_ref[...], weight_ref[...], 1, 1).astype(out_ref.dtype)


def piece_products(weights, rows, pieces):
    row_count, depth = rows.shape
    columns = weights.shape[0] // pieces
    tile = row_count // 2
    return pl.pallas_call(
        piece_kernel,
        grid=(2, pieces),
        in_specs=[
            pl.BlockSpec((columns, depth), lambda i, j: (j, 0)),
            pl.BlockSpec((tile, depth), lambda i, j: (i, 0)),
        ],
        out_specs=pl.BlockSpec((None, tile, columns), lambda i, j: (j, i, 0)),
        out_shape=jax.ShapeDtypeStruct((pieces, row_count, columns), jnp.bfloat16),
        cost_estimate=pl.CostEstimate(
            flops=2 * row_count * depth * weights.shape[0],
            bytes_accessed=2 * (row_count * depth + weights.size + row_count * weights.shape[0]),
            transcendentals=0,
        ),
    )(weights, rows)


def halving(part, bit, left, axis):
    devices, me = lax.axis_size(axis), lax.axis_index(axis)
    at, weight = left.index(bit), devices.bit_length() - 2 - bit
    mine = lax.rem(me // (1 << weight), 2)
    kept = lax.dynamic_index_in_dim(part, mine, at, keepdims=False)
    sent = lax.dynamic_index_in_dim(part, 1 - mine, at, keepdims=False)
    return kept, lax.ppermute(sent, axis, [(i, i ^ (1 << weight)) for i in range(devices)])


def halved_start(pieces, axis):
    bits = lax.axis_size(axis).bit_length() - 1
    half = pieces.shape[1] // 2
    pairs = []
    for side in range(2):
        part = pieces[:, side * half : (side + 1) * half]
        part = part.reshape((2,) * bits + part.shape[1:])
        left = list(range(bits))
        pairs.append(halving(part, left[0] if side else left[-1], left, axis))
    return pairs


def halved_finish(pairs, axis):
    bits = lax.axis_size(axis).bit_length() - 1
    totals = []
    for side, (kept, got) in enumerate(pairs):
        order = list(range(bits)) if side else list(range(bits))[::-1]
        left = list(range(bits))
        for done, following in zip(order, order[1:]):
            part = (kept.astype(jnp.float32) + got.astype(jnp.float32)).astype(jnp.bfloat16)
            left.remove(done)
            kept, got = halving(part, following, left, axis)
        totals.append(kept.astype(jnp.float32) + got.astype(jnp.float32))
    return jnp.concatenate(totals, axis=0)


def on_device(frames, ln_gain, ln_bias, w_in, w_depth, bn_gain, bn_bias, w_out, lengths, grad_out):
    records, local_len, model_width = frames.shape
    shard_in = w_in.shape[0]
    channels = w_in.shape[2]
    tap_count = w_depth.shape[0]
    margin = (tap_count - 1) // 2
    width = -(-margin // 16) * 16
    first_tap = width - margin
    local_rows = records * local_len
    chan_start = lax.axis_index("chan") * channels
    position = lax.axis_index("ctx") * local_len + jnp.arange(local_len, dtype=jnp.int32)
    valid_mask = (position[None, :] < lengths[:, None]).astype(jnp.float32)[:, :, None]
    frame_count = jnp.sum(lengths.astype(jnp.float32))
    inputs = frames.astype(jnp.float32)
    ln_mean = jnp.mean(inputs, axis=-1, keepdims=True)
    centred = inputs - ln_mean
    ln_rstd = lax.rsqrt(jnp.mean(centred * centred, axis=-1, keepdims=True) + epsilon)
    ln_hat = centred * ln_rstd
    normed = (ln_hat * ln_gain + ln_bias).astype(jnp.bfloat16)
    normed_rows = normed.reshape(local_rows, model_width)
    chan_count = lax.axis_size("chan")
    w_in_all = gather_rows(w_in.reshape(shard_in, 2 * channels), "ctx")
    w_in_all, w_out = lax.optimization_barrier((w_in_all, w_out))
    projected = jnp.dot(normed_rows, w_in_all, preferred_element_type=jnp.float32)
    projected = projected.reshape(records, local_len, 2, channels)
    values = projected[:, :, 0]
    gate_vals = jax.nn.sigmoid(projected[:, :, 1])
    glu_out = (values * gate_vals * valid_mask).astype(jnp.bfloat16)
    padded = lax.optimization_barrier(padded_2(glu_out, (("ctx", 1),), width))
    depth_out = jnp.zeros((records, local_len, channels), jnp.float32)
    for offset in range(tap_count):
        at = first_tap + offset
        depth_out = depth_out + padded[:, at : at + local_len].astype(jnp.float32) * w_depth[offset]
    starts = jnp.arange(lax.axis_size("ctx"), dtype=jnp.int32) * local_len
    counts = jnp.sum(
        jnp.clip(lengths[None, :] - starts[:, None], 0, local_len).astype(jnp.float32), axis=1
    )
    own_count = jnp.maximum(
        jnp.sum(jnp.clip(lengths - starts[0] - lax.axis_index("ctx") * local_len, 0, local_len)), 1
    ).astype(jnp.float32)
    own_sum = jnp.sum(depth_out * valid_mask, axis=(0, 1))
    own_cent = (depth_out - own_sum / own_count) * valid_mask
    own_square = jnp.sum(own_cent * own_cent, axis=(0, 1))
    (stats,) = exchange(0, (jnp.stack([own_sum, own_square]), "ctx", False))
    sums, squares = stats[:, 0], stats[:, 1]
    bn_mean = jnp.sum(sums, axis=0) / frame_count
    shifts = sums / jnp.maximum(counts, 1.0)[:, None] - bn_mean
    bn_var = jnp.sum(squares + counts[:, None] * shifts * shifts, axis=0) / frame_count
    bn_rstd = lax.rsqrt(bn_var + epsilon)
    bn_hat = (depth_out - bn_mean) * bn_rstd
    bn_out = bn_hat * bn_gain + bn_bias
    swish_gate = jax.nn.sigmoid(bn_out)
    activated = (bn_out * swish_gate * valid_mask).astype(jnp.bfloat16)
    act_rows = activated.reshape(local_rows, channels)
    w_out_all = lax.all_gather(w_out, "ctx", axis=0, tiled=True)
    grad_rows = grad_out.reshape(local_rows, model_width)
    own_out = []
    late_grad = grad_rows
    for record in range(records):
        proj_out = piece_products(w_out_all, activated[record], chan_count)
        proj_out, late_grad = lax.optimization_barrier((proj_out, late_grad))
        own_out.append(halved_finish(halved_start(proj_out, "chan"), "chan"))
    own_out = jnp.concatenate(own_out, axis=0)
    own_frames = lax.dynamic_slice_in_dim(
        frames.reshape(local_rows, model_width), chan_start, channels, 1
    ).astype(jnp.float32)
    block_out = (own_frames + own_out).astype(jnp.bfloat16)
    block_out = block_out.reshape(records, local_len, channels)
    grad_act = jnp.dot(late_grad, w_out_all, preferred_element_type=jnp.float32)
    grad_act = grad_act.reshape(records, local_len, channels)
    grad_bn_out = grad_act * valid_mask * (swish_gate * (1.0 + bn_out * (1.0 - swish_gate)))
    own_grad_bn = jnp.stack(
        [jnp.sum(grad_bn_out * bn_hat, axis=(0, 1)), jnp.sum(grad_bn_out, axis=(0, 1))]
    )
    (grad_bn,) = exchange(1, (own_grad_bn, "ctx", True))
    gain_sum, bias_sum = grad_bn[0], grad_bn[1]
    grad_depth = (
        valid_mask
        * (bn_gain * bn_rstd)
        * (grad_bn_out - (bias_sum + bn_hat * gain_sum) / frame_count)
    )
    grad_padded = lax.optimization_barrier(padded_2(grad_depth, (("ctx", 1),), width))
    own_grad, grad_proj = [], []
    late_padded = [grad_padded[record] for record in range(records)]
    for record in range(records):
        grad_glu = jnp.zeros((local_len, channels), jnp.float32)
        for offset in range(tap_count):
            at = first_tap + tap_count - 1 - offset
            grad_glu = grad_glu + late_padded[record][at : at + local_len] * w_depth[offset]
        grad_glu = grad_glu * valid_mask[record]
        gate = gate_vals[record]
        proj_record = jnp.concatenate(
            [
                (grad_glu * gate).astype(jnp.bfloat16),
                (grad_glu * values[record] * gate * (1.0 - gate)).astype(jnp.bfloat16),
            ],
            axis=1,
        )
        grad_part = piece_products(w_in_all, proj_record, chan_count)
        if record + 1 < records:
            grad_part, late_padded[record + 1] = lax.optimization_barrier(
                (grad_part, late_padded[record + 1])
            )
        grad_proj.append(proj_record)
        own_grad.append(halved_start(grad_part, "chan"))
    grad_proj = jnp.concatenate(grad_proj, axis=0)
    own_grad[0], act_rows, normed_rows, grad_proj, grad_depth, padded = lax.optimization_barrier(
        (own_grad[0], act_rows, normed_rows, grad_proj, grad_depth, padded)
    )
    own_grad = jnp.concatenate([halved_finish(pairs, "chan") for pairs in own_grad], axis=0)
    grad_w_in = scatter_sum(contract(normed_rows, grad_proj, 0, 0).astype(jnp.bfloat16), "ctx")
    grad_w_in = grad_w_in.reshape(shard_in, 2, channels)
    grad_w_out = scatter_sum(contract(grad_rows, act_rows, 0, 0).astype(jnp.bfloat16), "ctx")
    depth_local = jnp.stack(
        [
            jnp.sum(
                grad_depth
                * padded[:, first_tap + offset : first_tap + offset + local_len].astype(jnp.float32),
                axis=(0, 1),
            )
            for offset in range(tap_count)
        ]
    )
    (grad_w_depth,) = exchange(2, (depth_local, "ctx", True))
    rstd_rows = ln_rstd.reshape(local_rows, 1)
    own_hat = (own_frames - ln_mean.reshape(local_rows, 1)) * rstd_rows
    own_gain = lax.dynamic_slice_in_dim(ln_gain, chan_start, channels, 0)
    own_scaled = own_grad * own_gain
    row_sums, grad_ln = exchange(
        3,
        (jnp.stack([jnp.sum(own_scaled, axis=1), jnp.sum(own_scaled * own_hat, axis=1)]), "chan", True),
        (jnp.stack([jnp.sum(own_grad * own_hat, axis=0), jnp.sum(own_grad, axis=0)]), "ctx", True),
    )
    first_rows, second_rows = row_sums[0], row_sums[1]
    own_dx = rstd_rows * (
        own_scaled
        - first_rows[:, None] / model_width
        - own_hat * (second_rows[:, None] / model_width)
    )
    own_cotangent = lax.dynamic_slice_in_dim(grad_rows, chan_start, channels, 1).astype(jnp.float32)
    grad_frames = (
        (own_dx + own_cotangent).astype(jnp.bfloat16).reshape(records, local_len, channels)
    )
    return (block_out, grad_frames, grad_w_in, grad_w_out, grad_w_depth, grad_bn, grad_ln)


def solution(mesh):
    in_specs = (
        P(None, "ctx", None),
        P(),
        P(),
        P("ctx", None, "chan"),
        P(None, "chan"),
        P("chan"),
        P("chan"),
        P("ctx", "chan"),
        P(),
        P(None, "ctx", None),
    )
    out_specs = (
        P(None, "ctx", "chan"),
        P(None, "ctx", "chan"),
        P("ctx", None, "chan"),
        P("ctx", "chan"),
        P(None, "chan"),
        P(None, "chan"),
        P(None, "chan"),
    )
    return jax.shard_map(
        on_device, mesh=mesh, in_specs=in_specs, out_specs=out_specs, check_vma=False
    )
```

```python
import functools

import jax
import jax.numpy as jnp
from jax import lax
from jax.experimental import pallas as pl
from jax.experimental.pallas import tpu as pltpu
from jax.sharding import PartitionSpec as P

epsilon = 1e-05


def padded_2(shard, sides, width):
    for axis, dim in sides:
        devices, length = (lax.axis_size(axis), shard.shape[dim])
        up = [(i, (i + 1) % devices) for i in range(devices - 1)]
        down = [(j, i) for i, j in up]
        last = lax.slice_in_dim(shard, length - width, length, axis=dim)
        initial = lax.slice_in_dim(shard, 0, width, axis=dim)
        before = lax.ppermute(last, axis, up)
        after = lax.ppermute(initial, axis, down)
        shard = jnp.concatenate([before, shard, after], axis=dim)
    return shard


def contract(left_op, right_op, left_dim, right_dim):
    return lax.dot_general(
        left_op,
        right_op,
        (((left_dim,), (right_dim,)), ((), ())),
        preferred_element_type=jnp.float32,
    )


def exchange_kernel(axes, summed, *refs):
    count = len(axes)
    inputs, outputs, slots = refs[:count], refs[count : 2 * count], refs[2 * count : 3 * count]
    send_sem, recv_sem = refs[3 * count :]
    barrier = pltpu.get_barrier_semaphore()
    greeted = 0
    for axis in sorted(set(axes)):
        devices, me = lax.axis_size(axis), lax.axis_index(axis)
        for step in range(1, devices):
            pl.semaphore_signal(
                barrier,
                inc=1,
                device_id={axis: lax.rem(me + step, devices)},
                device_id_type=pl.DeviceIdType.MESH,
            )
            greeted += 1
    pl.semaphore_wait(barrier, greeted)
    copies = []
    for axis, source, landing in zip(axes, inputs, slots):
        devices, me = lax.axis_size(axis), lax.axis_index(axis)
        for step in range(1, devices):
            copy = pltpu.make_async_remote_copy(
                src_ref=source,
                dst_ref=landing.at[me],
                send_sem=send_sem.at[len(copies)],
                recv_sem=recv_sem.at[len(copies)],
                device_id={axis: lax.rem(me + step, devices)},
                device_id_type=pl.DeviceIdType.MESH,
            )
            copy.start()
            copies.append(copy)
    for axis, source, landing in zip(axes, inputs, slots):
        landing[lax.axis_index(axis)] = source[...]
    for copy in copies:
        copy.wait_recv()
    for add_up, landing, output in zip(summed, slots, outputs):
        if add_up:
            total = landing[0]
            for place in range(1, landing.shape[0]):
                total = total + landing[place]
            output[...] = total
        else:
            output[...] = landing[...]
    for copy in copies:
        copy.wait_send()


def exchange(collective_id, *operands):
    arrays = [array for array, _, _ in operands]
    axes = tuple(axis for _, axis, _ in operands)
    summed = tuple(add_up for _, _, add_up in operands)
    stacked = [(lax.axis_size(axis),) + array.shape for array, axis, _ in operands]
    copies = sum(lax.axis_size(axis) - 1 for axis in axes)
    vmem = pl.BlockSpec(memory_space=pltpu.VMEM)
    return pl.pallas_call(
        functools.partial(exchange_kernel, axes, summed),
        out_shape=[
            jax.ShapeDtypeStruct(array.shape if add_up else shape, array.dtype)
            for array, shape, add_up in zip(arrays, stacked, summed)
        ],
        in_specs=[vmem] * len(arrays),
        out_specs=[vmem] * len(arrays),
        scratch_shapes=[
            pltpu.VMEM(shape, array.dtype) for array, shape in zip(arrays, stacked)
        ]
        + [pltpu.SemaphoreType.DMA((copies,)), pltpu.SemaphoreType.DMA((copies,))],
        compiler_params=pltpu.CompilerParams(collective_id=collective_id, has_side_effects=True),
    )(*arrays)


def scatter_sum(whole, axis):
    devices, me = lax.axis_size(axis), lax.axis_index(axis)
    chips, core, chip = devices // 2, lax.rem(me, 2), me // 2
    pieces = whole.reshape((chips, 2, whole.shape[0] // devices) + whole.shape[1:])
    kept = lax.dynamic_index_in_dim(pieces, core, 1, keepdims=False)
    sent = lax.dynamic_index_in_dim(pieces, 1 - core, 1, keepdims=False)
    got = lax.ppermute(sent, axis, [(i, i ^ 1) for i in range(devices)])
    pair = kept.astype(jnp.float32) + got.astype(jnp.float32)
    total = lax.dynamic_index_in_dim(pair, chip, 0, keepdims=False)
    rounded = pair.astype(jnp.bfloat16)
    for step in range(1, chips):
        part = lax.dynamic_index_in_dim(rounded, lax.rem(chip + step, chips), 0, keepdims=False)
        ring = [(i, ((i // 2 + step) % chips) * 2 + i % 2) for i in range(devices)]
        total = total + lax.ppermute(part, axis, ring).astype(jnp.float32)
    return total


def piece_kernel(weight_ref, rows_ref, out_ref):
    out_ref[...] = contract(rows_ref[...], weight_ref[...], 1, 1).astype(out_ref.dtype)


def piece_products(weights, rows, pieces):
    row_count, depth = rows.shape
    columns = weights.shape[0] // pieces
    tile = row_count // 2
    return pl.pallas_call(
        piece_kernel,
        grid=(2, pieces),
        in_specs=[
            pl.BlockSpec((columns, depth), lambda i, j: (j, 0)),
            pl.BlockSpec((tile, depth), lambda i, j: (i, 0)),
        ],
        out_specs=pl.BlockSpec((None, tile, columns), lambda i, j: (j, i, 0)),
        out_shape=jax.ShapeDtypeStruct((pieces, row_count, columns), jnp.bfloat16),
        cost_estimate=pl.CostEstimate(
            flops=2 * row_count * depth * weights.shape[0],
            bytes_accessed=2 * (row_count * depth + weights.size + row_count * weights.shape[0]),
            transcendentals=0,
        ),
    )(weights, rows)


def on_device(frames, ln_gain, ln_bias, w_in, w_depth, bn_gain, bn_bias, w_out, lengths, grad_out):
    records, local_len, model_width = frames.shape
    shard_in = w_in.shape[0]
    channels = w_in.shape[2]
    tap_count = w_depth.shape[0]
    margin = (tap_count - 1) // 2
    width = -(-margin // 16) * 16
    first_tap = width - margin
    local_rows = records * local_len
    chan_start = lax.axis_index("chan") * channels
    position = lax.axis_index("ctx") * local_len + jnp.arange(local_len, dtype=jnp.int32)
    valid_mask = (position[None, :] < lengths[:, None]).astype(jnp.float32)[:, :, None]
    frame_count = jnp.sum(lengths.astype(jnp.float32))
    inputs = frames.astype(jnp.float32)
    ln_mean = jnp.mean(inputs, axis=-1, keepdims=True)
    centred = inputs - ln_mean
    ln_rstd = lax.rsqrt(jnp.mean(centred * centred, axis=-1, keepdims=True) + epsilon)
    ln_hat = centred * ln_rstd
    normed = (ln_hat * ln_gain + ln_bias).astype(jnp.bfloat16)
    normed_rows = normed.reshape(local_rows, model_width)
    w_in_all = lax.all_gather(
        w_in.reshape(shard_in, 2 * channels), "ctx", axis=0, tiled=True
    )
    projected = jnp.dot(normed_rows, w_in_all, preferred_element_type=jnp.float32)
    projected = projected.reshape(records, local_len, 2, channels)
    values = projected[:, :, 0]
    gate_vals = jax.nn.sigmoid(projected[:, :, 1])
    glu_out = (values * gate_vals * valid_mask).astype(jnp.bfloat16)
    padded = lax.optimization_barrier(padded_2(glu_out, (("ctx", 1),), width))
    depth_out = jnp.zeros((records, local_len, channels), jnp.float32)
    for offset in range(tap_count):
        at = first_tap + offset
        depth_out = depth_out + padded[:, at : at + local_len].astype(jnp.float32) * w_depth[offset]
    starts = jnp.arange(lax.axis_size("ctx"), dtype=jnp.int32) * local_len
    counts = jnp.sum(
        jnp.clip(lengths[None, :] - starts[:, None], 0, local_len).astype(jnp.float32), axis=1
    )
    own_count = jnp.maximum(
        jnp.sum(jnp.clip(lengths - starts[0] - lax.axis_index("ctx") * local_len, 0, local_len)), 1
    ).astype(jnp.float32)
    own_sum = jnp.sum(depth_out * valid_mask, axis=(0, 1))
    own_cent = (depth_out - own_sum / own_count) * valid_mask
    own_square = jnp.sum(own_cent * own_cent, axis=(0, 1))
    (stats,) = exchange(0, (jnp.stack([own_sum, own_square]), "ctx", False))
    sums, squares = stats[:, 0], stats[:, 1]
    bn_mean = jnp.sum(sums, axis=0) / frame_count
    shifts = sums / jnp.maximum(counts, 1.0)[:, None] - bn_mean
    bn_var = jnp.sum(squares + counts[:, None] * shifts * shifts, axis=0) / frame_count
    bn_rstd = lax.rsqrt(bn_var + epsilon)
    bn_hat = (depth_out - bn_mean) * bn_rstd
    bn_out = bn_hat * bn_gain + bn_bias
    swish_gate = jax.nn.sigmoid(bn_out)
    activated = (bn_out * swish_gate * valid_mask).astype(jnp.bfloat16)
    act_rows = activated.reshape(local_rows, channels)
    w_out_all = lax.all_gather(w_out, "ctx", axis=0, tiled=True)
    grad_rows = grad_out.reshape(local_rows, model_width)
    proj_out = piece_products(w_out_all, act_rows, lax.axis_size("chan"))
    proj_out, late_grad = lax.optimization_barrier((proj_out, grad_rows))
    own_out = lax.psum_scatter(proj_out, "chan", scatter_dimension=0, tiled=True)[0]
    own_frames = lax.dynamic_slice_in_dim(
        frames.reshape(local_rows, model_width), chan_start, channels, 1
    ).astype(jnp.float32)
    grad_act = jnp.dot(late_grad, w_out_all, preferred_element_type=jnp.float32)
    grad_act = grad_act.reshape(records, local_len, channels)
    grad_bn_out = grad_act * valid_mask * (swish_gate * (1.0 + bn_out * (1.0 - swish_gate)))
    own_grad_bn = jnp.stack(
        [jnp.sum(grad_bn_out * bn_hat, axis=(0, 1)), jnp.sum(grad_bn_out, axis=(0, 1))]
    )
    (grad_bn,) = exchange(1, (own_grad_bn, "ctx", True))
    gain_sum, bias_sum = grad_bn[0], grad_bn[1]
    grad_depth = (
        valid_mask
        * (bn_gain * bn_rstd)
        * (grad_bn_out - (bias_sum + bn_hat * gain_sum) / frame_count)
    )
    grad_padded = lax.optimization_barrier(padded_2(grad_depth, (("ctx", 1),), width))
    grad_glu = jnp.zeros((records, local_len, channels), jnp.float32)
    for offset in range(tap_count):
        at = first_tap + tap_count - 1 - offset
        grad_glu = grad_glu + grad_padded[:, at : at + local_len] * w_depth[offset]
    grad_glu = grad_glu * valid_mask
    grad_values = grad_glu * gate_vals
    grad_gates = grad_glu * values * gate_vals * (1.0 - gate_vals)
    grad_proj = jnp.concatenate(
        [
            grad_values.astype(jnp.bfloat16).reshape(local_rows, channels),
            grad_gates.astype(jnp.bfloat16).reshape(local_rows, channels),
        ],
        axis=1,
    )
    grad_part = piece_products(w_in_all, grad_proj, lax.axis_size("chan"))
    grad_part, act_rows, normed_rows, grad_proj, grad_depth, padded = lax.optimization_barrier(
        (grad_part, act_rows, normed_rows, grad_proj, grad_depth, padded)
    )
    grad_part, own_out = lax.optimization_barrier((grad_part, own_out))
    own_grad = lax.psum_scatter(grad_part, "chan", scatter_dimension=0, tiled=True)
    own_grad = own_grad[0].astype(jnp.float32)
    grad_w_in = scatter_sum(contract(normed_rows, grad_proj, 0, 0).astype(jnp.bfloat16), "ctx")
    grad_w_in = grad_w_in.reshape(shard_in, 2, channels)
    grad_w_out = scatter_sum(contract(grad_rows, act_rows, 0, 0).astype(jnp.bfloat16), "ctx")
    depth_local = jnp.stack(
        [
            jnp.sum(
                grad_depth
                * padded[:, first_tap + offset : first_tap + offset + local_len].astype(jnp.float32),
                axis=(0, 1),
            )
            for offset in range(tap_count)
        ]
    )
    (grad_w_depth,) = exchange(2, (depth_local, "ctx", True))
    rstd_rows = ln_rstd.reshape(local_rows, 1)
    own_hat = (own_frames - ln_mean.reshape(local_rows, 1)) * rstd_rows
    own_gain = lax.dynamic_slice_in_dim(ln_gain, chan_start, channels, 0)
    own_scaled = own_grad * own_gain
    row_sums, grad_ln = exchange(
        3,
        (jnp.stack([jnp.sum(own_scaled, axis=1), jnp.sum(own_scaled * own_hat, axis=1)]), "chan", True),
        (jnp.stack([jnp.sum(own_grad * own_hat, axis=0), jnp.sum(own_grad, axis=0)]), "ctx", True),
    )
    first_rows, second_rows = row_sums[0], row_sums[1]
    own_dx = rstd_rows * (
        own_scaled
        - first_rows[:, None] / model_width
        - own_hat * (second_rows[:, None] / model_width)
    )
    own_cotangent = lax.dynamic_slice_in_dim(grad_rows, chan_start, channels, 1).astype(jnp.float32)
    grad_frames = (
        (own_dx + own_cotangent).astype(jnp.bfloat16).reshape(records, local_len, channels)
    )
    block_out = (own_frames + own_out.astype(jnp.float32)).astype(jnp.bfloat16)
    block_out = block_out.reshape(records, local_len, channels)
    return (block_out, grad_frames, grad_w_in, grad_w_out, grad_w_depth, grad_bn, grad_ln)


def solution(mesh):
    in_specs = (
        P(None, "ctx", None),
        P(),
        P(),
        P("ctx", None, "chan"),
        P(None, "chan"),
        P("chan"),
        P("chan"),
        P("ctx", "chan"),
        P(),
        P(None, "ctx", None),
    )
    out_specs = (
        P(None, "ctx", "chan"),
        P(None, "ctx", "chan"),
        P("ctx", None, "chan"),
        P("ctx", "chan"),
        P(None, "chan"),
        P(None, "chan"),
        P(None, "chan"),
    )
    return jax.shard_map(
        on_device, mesh=mesh, in_specs=in_specs, out_specs=out_specs, check_vma=False
    )
```
